32 devices in a mesh: wide: 2 (over core), op: 16 (over z, y, x).
Axes of the slice: x: 2, y: 2, z: 4, core: 2. Of those that a mesh axis runs over, the one named last changes fastest.
Arguments:
- wavefunction: bfloat16 [32, 4, 512, 512], P('wide', None, 'op'), may hold values from -6 to 6
- left_ops: bfloat16 [128, 512, 512], P(('wide', 'op')), may hold values from -0.0390625 to 0.0390625
- right_ops: bfloat16 [128, 512, 512], P(('wide', 'op')), may hold values from -0.25 to 0.25
- in_sector: int32 [128], P(('wide', 'op')), may hold values from 0 to 31
- live_count: int32 [32], P(('wide', 'op')), may hold values from 2 to 4, as said below
Outputs:
- sigma_blocks: bfloat16 [2, 4, 512, 512], P('wide', None, 'op')
The draws below stay inside these ranges and needn't reach their ends.
Inputs may be any that keep to these rules, and one draw needn't show every extreme that they name: `live_count`: in each aligned group of 16 entries (the devices of one op group), entries i and i + 8 sum to 6, and exactly 4 entries are 4.
All inputs are finite; a program needn't handle non-finite values.
Results may differ from the reference program's by a relative error of at most 0.0065.
Values may be sent and summed in bfloat16 or wider, within the bound.
A program may use at most 64 MiB of HBM per device.

```python
import jax
import jax.numpy as jnp
from jax import lax

M = 512
S = 4
SLOTS = 4
SECT = 32
TASKS = 128
N_WIDE = 2
N_OP = 16


def draw_live_count(key, part):
    half_size = N_OP // 2
    heavy_count = N_OP // 4
    subkeys = jax.random.split(jax.random.fold_in(key, 7), N_WIDE)

    def one_group(subkey):
        order_key, side_key = jax.random.split(subkey)
        ranked = jax.random.permutation(order_key, jnp.arange(half_size, dtype=jnp.int32))
        side = jax.random.randint(side_key, (half_size,), 0, 2).astype(jnp.int32)
        first = jnp.where(ranked < heavy_count, jnp.where(side == 1, 4, 2), 3).astype(jnp.int32)
        second = (6 - first).astype(jnp.int32)
        return jnp.concatenate([first, second])
    return jax.vmap(one_group)(subkeys).reshape(-1).astype(jnp.int32)


def with_ends(drawn, stream_key, smallest, high):
    extent = drawn.shape
    place = [jax.random.randint(jax.random.fold_in(stream_key, axis), (), 0, extent[axis]) for axis in range(len(extent))]
    drawn = drawn.at[tuple(place)].set(smallest)
    longest = extent.index(max(extent))
    place[longest] = (place[longest] + 1) % extent[longest]
    return drawn.at[tuple(place)].set(high)


def block_levels(stream_key, dims, pieces, smallest, top_value):
    def one(axis_at, blocks):
        draws = jax.random.uniform(jax.random.fold_in(jax.random.fold_in(stream_key, 6), axis_at), (blocks,), jnp.float32, smallest / len(pieces), top_value / len(pieces))
        return jnp.repeat(jnp.exp(draws), dims[axis_at] // blocks).reshape((-1,) + (1,) * (len(dims) - axis_at - 1))

    loudness = one(*pieces[0])
    for cut in pieces[1:]:
        loudness = loudness * one(*cut)
    return loudness


def centred(stream_key, dims, deviation, bound, cuts=(), kind=jnp.bfloat16):
    entries = deviation * jax.random.normal(stream_key, dims, jnp.float32)
    if cuts:
        entries = entries * block_levels(stream_key, dims, cuts, -0.22, 0.18)
    return jnp.clip(entries, -bound, bound).astype(kind)


def setup_inputs(seed: int = 0) -> dict:
    arg_keys = jax.random.split(jax.random.key(seed), 6)
    wavefunction = centred(arg_keys[0], (SECT, S, M, M), 1.0, 6.0, ((0, 2), (2, 16)))
    left_ops = centred(arg_keys[1], (TASKS, M, M), (3 * M * N_OP) ** -0.5, 0.0390625, ((0, 32),))
    right_ops = centred(arg_keys[2], (TASKS, M, M), M ** -0.5, 0.25, ((0, 32),))
    in_sector = with_ends(jax.random.randint(arg_keys[3], (TASKS,), 0, SECT), jax.random.fold_in(arg_keys[3], 1), 0, SECT - 1).astype(jnp.int32)
    live_count = draw_live_count(jax.random.fold_in(arg_keys[5], 71), 0)
    return dict(wavefunction=wavefunction, left_ops=left_ops, right_ops=right_ops, in_sector=in_sector, live_count=live_count)


def sandwich(sector, left_op, right_op):
    half_step = jnp.einsum("smk,nk->smn", sector.astype(jnp.float32), right_op.astype(jnp.float32))
    half_step = lax.optimization_barrier(half_step.astype(jnp.bfloat16)).astype(jnp.float32)
    return jnp.einsum("im,smn->sin", left_op.astype(jnp.float32), half_step)


def reference(wavefunction, left_ops, right_ops, in_sector, live_count):
    slot_count = SLOTS
    device_total = live_count.shape[0]

    def visit(sigma_acc, device_id):
        partial_value = jnp.zeros(wavefunction.shape[1:], jnp.float32)
        for slot_index in range(slot_count):
            task_id = (device_id * slot_count + slot_index).astype(jnp.int32)
            sector = lax.dynamic_index_in_dim(wavefunction, in_sector[task_id].astype(jnp.int32), 0, keepdims=False)
            left_op = lax.dynamic_index_in_dim(left_ops, task_id, 0, keepdims=False)
            right_op = lax.dynamic_index_in_dim(right_ops, task_id, 0, keepdims=False)
            weight = (slot_index < live_count[device_id]).astype(jnp.float32)
            partial_value = partial_value + weight * sandwich(sector, left_op, right_op)
        owner = (device_id // N_OP).astype(jnp.int32)
        current = lax.dynamic_index_in_dim(sigma_acc, owner, 0, keepdims=False)
        sigma_acc = lax.dynamic_update_index_in_dim(sigma_acc, current + partial_value, owner, 0)
        return sigma_acc, None

    sigma_acc = jnp.zeros((N_WIDE,) + wavefunction.shape[1:], jnp.float32)
    sigma_acc, unused = lax.scan(visit, sigma_acc, jnp.arange(device_total, dtype=jnp.int32))
    return sigma_acc.astype(jnp.bfloat16)
```

```python
import jax
import jax.numpy as jnp
from jax import lax
from jax.sharding import PartitionSpec as P


def sandwich(sector, left_op, right_op):
    half_step = jnp.einsum(
        "smk,nk->smn", sector, right_op, preferred_element_type=jnp.float32
    ).astype(jnp.bfloat16)
    return jnp.einsum("im,smn->sin", left_op, half_step, preferred_element_type=jnp.float32)


def work_list(live, mine, theirs):
    third = jnp.where(live >= 3, mine[2], theirs[2])
    fourth = jnp.where(live >= 4, mine[3], jnp.where(live == 3, theirs[2], theirs[3]))
    return [mine[0], mine[1], theirs[0], theirs[1], third, fourth]


def local(wavefunction, left_ops, right_ops, in_sector, live_count):
    n = lax.axis_size("op")
    half_n = n // 2
    slots, size = left_ops.shape[0], left_ops.shape[1]
    me = lax.axis_index("op")
    side = me // half_n
    swap = [(i, (i + half_n) % n) for i in range(n)]
    split = size // 2
    left_mine = lax.dynamic_slice_in_dim(left_ops, side * split, split, axis=2)
    left_away = lax.dynamic_slice_in_dim(left_ops, (1 - side) * split, split, axis=2)
    right_theirs = lax.ppermute(right_ops, "op", swap)
    left_theirs = lax.ppermute(left_away, "op", swap)

    small = lax.all_gather(jnp.concatenate([in_sector, live_count]), "op", axis=0)
    ins, live = small[:, :slots], small[:, slots]
    rows = lax.all_gather(wavefunction, "wide", axis=0, tiled=True)
    partner = jnp.roll(ins, half_n, axis=0)
    grid = jnp.stack(work_list(live, ins.T, partner.T), axis=1)
    grid = lax.dynamic_slice_in_dim(grid, side * half_n, half_n, axis=0)
    outgoing = jnp.take(rows, grid.reshape(-1), axis=0)
    groups = [list(range(half_n)), list(range(half_n, n))]
    arrived = lax.all_to_all(
        outgoing, "op", split_axis=0, concat_axis=2, tiled=True, axis_index_groups=groups
    )
    lefts = work_list(live_count[0], left_mine, left_theirs)
    rights = work_list(live_count[0], right_ops, right_theirs)
    total = None
    for t in range(len(lefts)):
        term = sandwich(arrived[t], lefts[t], rights[t])
        total = term if total is None else total + term
    pieces = lax.all_to_all(
        total.astype(jnp.bfloat16).reshape(total.shape[0], n, size // n, size),
        "op", split_axis=1, concat_axis=1, tiled=True,
    )
    return jnp.sum(pieces.astype(jnp.float32), axis=1).astype(jnp.bfloat16)[None]


def solution(mesh):
    placed = (
        P("wide", None, "op", None),
        P(("wide", "op"), None, None),
        P(("wide", "op"), None, None),
        P(("wide", "op")),
        P(("wide", "op")),
    )
    return jax.shard_map(
        local, mesh=mesh, in_specs=placed, out_specs=P("wide", None, "op", None), check_vma=False
    )
```

```python
import functools

import jax
import jax.numpy as jnp
from jax import lax
from jax.experimental import pallas as pl
from jax.experimental.pallas import tpu as pltpu
from jax.sharding import PartitionSpec as P

MESH = pl.DeviceIdType.MESH
WORK = 6


def work_list(live, mine, theirs):
    third = jnp.where(live >= 3, mine[2], theirs[2])
    fourth = jnp.where(live >= 4, mine[3], jnp.where(live == 3, theirs[2], theirs[3]))
    return [mine[0], mine[1], theirs[0], theirs[1], third, fourth]


def kernel(
    n, wides, table, wf, lefts, rights, out,
    rows, outgoing, arrived, left_v, right_v, acc, red_out, red_in, swap_out, swap_in,
    local_sem, wide_sem, op_send, op_recv, a2a_send, a2a_recv, red_send, red_recv, swap_sem,
):
    h = n // 2
    w = lax.axis_index("wide")
    me = lax.axis_index("op")
    side = lax.div(me, h)
    r = lax.rem(me, h)
    base = side * h
    partner = lax.rem(me + h, n)
    sectors, states, depth, size = wf.shape
    slots = lefts.shape[0]
    split = size // 2

    barrier = pltpu.get_barrier_semaphore()

    def greet(k, c):
        to = base + lax.rem(r + k, h)
        pl.semaphore_signal(barrier, inc=1, device_id=(w, to), device_id_type=MESH)
        return c

    other = 1 - w
    pl.semaphore_signal(barrier, inc=1, device_id=(w, partner), device_id_type=MESH)
    pl.semaphore_signal(barrier, inc=1, device_id=(other, me), device_id_type=MESH)
    lax.fori_loop(1, h, greet, 0)

    my_cols = pl.ds(pl.multiple_of(side * split, split), split)
    away_cols = pl.ds(pl.multiple_of((1 - side) * split, split), split)
    my_sectors = pl.ds(w * sectors, sectors)
    own_rows = pltpu.make_async_copy(wf, rows.at[my_sectors], local_sem.at[0])
    own_right = pltpu.make_async_copy(rights, right_v.at[pl.ds(0, slots)], local_sem.at[1])
    own_left = pltpu.make_async_copy(
        lefts.at[:, :, my_cols], left_v.at[pl.ds(0, slots)], local_sem.at[2]
    )
    own_rows.start()
    own_right.start()
    own_left.start()
    pl.semaphore_wait(barrier, h + 1)

    def remote(src, dst, ssem, rsem, to):
        return pltpu.make_async_remote_copy(
            src_ref=src, dst_ref=dst, send_sem=ssem, recv_sem=rsem,
            device_id=to, device_id_type=MESH,
        )

    wide_copy = remote(wf, rows.at[my_sectors], wide_sem.at[0], wide_sem.at[1], (other, me))
    wide_copy.start()
    right_copies = [
        remote(rights.at[j], right_v.at[slots + j], op_send.at[0, j], op_recv.at[0, j], (w, partner))
        for j in range(slots)
    ]
    left_copies = [
        remote(
            lefts.at[j, :, away_cols], left_v.at[slots + j],
            op_send.at[1, j], op_recv.at[1, j], (w, partner),
        )
        for j in range(slots)
    ]
    right_copies[0].start()
    left_copies[0].start()
    own_rows.wait()
    wide_copy.wait()

    def fill(t):
        def one(e, c):
            outgoing[t, e] = rows[table[e * WORK + t]]
            return c

        lax.fori_loop(0, h, one, 0)
        arrived[t, r] = rows[table[h * WORK + 2 + t]]

    def a2a(t, k):
        e = lax.rem(r + k, h)
        return remote(
            outgoing.at[t, e], arrived.at[t, r], a2a_send.at[t, e], a2a_recv.at[t, r], (w, base + e)
        )

    def a2a_from(t, k):
        e = lax.rem(r + k, h)
        return remote(
            outgoing.at[t, e], arrived.at[t, e], a2a_send.at[t, e], a2a_recv.at[t, e], (w, base + e)
        )

    def each(action):
        def step(k, c):
            action(k)
            return c

        lax.fori_loop(1, h, step, 0)

    for t in range(WORK):
        fill(t)
        if t:
            each(lambda k: a2a(t - 1, k).start())
    each(lambda k: a2a(WORK - 1, k).start())
    for j in range(1, slots):
        right_copies[j].start()
        left_copies[j].start()

    def compute(t, at, first=False):
        def one(s, c):
            x = arrived[t, :, s]
            if depth % 16:
                x = x.astype(jnp.float32)
            x = x.reshape(h * depth, size).astype(jnp.bfloat16)
            half = lax.dot_general(
                x, right_v[at], (((1,), (1,)), ((), ())), preferred_element_type=jnp.float32
            ).astype(jnp.bfloat16)
            term = jnp.dot(left_v[at], half, preferred_element_type=jnp.float32)
            acc[s] = term if first else acc[s] + term
            return c

        lax.fori_loop(0, states, one, 0)

    own_right.wait()
    own_left.wait()
    for t in range(2):
        each(lambda k: a2a_from(t, k).wait_recv())
        compute(t, t, first=t == 0)
    for t in range(2, 4):
        each(lambda k: a2a_from(t, k).wait_recv())
        right_copies[t - 2].wait_recv()
        left_copies[t - 2].wait_recv()
        compute(t, slots + t - 2)
    for t in range(4, WORK):
        each(lambda k: a2a_from(t, k).wait_recv())
    for j in range(2, slots):
        right_copies[j].wait_recv()
        left_copies[j].wait_recv()
    for t in range(4, WORK):
        compute(t, table[h * WORK + t - 4])

    def pack(e, c):
        for p in range(2):
            at = pl.ds(pl.multiple_of((p * h + e) * depth, depth), depth)
            red_out[e, p] = acc[:, at, :].astype(jnp.bfloat16)
        return c

    def red(k):
        e = lax.rem(r + k, h)
        return remote(red_out.at[e], red_in.at[r], red_send.at[e], red_recv.at[r], (w, base + e))

    def red_from(k):
        e = lax.rem(r + k, h)
        return remote(red_out.at[e], red_in.at[e], red_send.at[e], red_recv.at[e], (w, base + e))

    lax.fori_loop(0, h, pack, 0)
    each(lambda k: red(k).start())
    each(lambda k: red_from(k).wait_recv())

    def mine(p):
        at = pl.ds(pl.multiple_of((p * h + r) * depth, depth), depth)
        start = acc[:, at, :]

        def add(k, total):
            return total + red_in[lax.rem(r + k, h), p].astype(jnp.float32)

        return lax.fori_loop(1, h, add, start)

    swap_out[...] = mine(1 - side).astype(jnp.bfloat16)
    swap = remote(swap_out, swap_in, swap_sem.at[0], swap_sem.at[1], (w, partner))
    swap.start()
    kept = mine(side)
    swap.wait()
    out[...] = (kept + swap_in[...].astype(jnp.float32)).astype(jnp.bfloat16)
    for t in range(WORK):
        each(lambda k: a2a(t, k).wait_send())
    each(lambda k: red(k).wait_send())
    for j in range(slots):
        right_copies[j].wait_send()
        left_copies[j].wait_send()


def local(wavefunction, left_ops, right_ops, in_sector, live_count):
    n, wides = lax.axis_size("op"), lax.axis_size("wide")
    h = n // 2
    slots, size = left_ops.shape[0], left_ops.shape[1]
    sectors, states, depth, _ = wavefunction.shape
    me = lax.axis_index("op")
    side, r = me // h, me % h
    small = lax.all_gather(jnp.concatenate([in_sector, live_count]), "op", axis=0)
    ins, live = small[:, :slots], small[:, slots]
    grid = jnp.stack(work_list(live, ins.T, jnp.roll(ins, h, axis=0).T), axis=1)
    grid = lax.dynamic_slice_in_dim(grid, side * h, h, axis=0)
    my_live = live_count[0]
    third = jnp.where(my_live >= 3, 2, slots + 2)
    fourth = jnp.where(my_live >= 4, 3, jnp.where(my_live == 3, slots + 2, slots + 3))
    own = lax.dynamic_index_in_dim(grid, r, 0, keepdims=False)
    table = jnp.concatenate([grid.reshape(-1), jnp.stack([third, fourth]), own]).astype(jnp.int32)
    dma = pltpu.SemaphoreType.DMA
    half_size = size // 2
    out = pl.pallas_call(
        functools.partial(kernel, n, wides),
        out_shape=jax.ShapeDtypeStruct((states, depth, size), jnp.bfloat16),
        in_specs=[pl.BlockSpec(memory_space=pltpu.SMEM)]
        + [pl.BlockSpec(memory_space=pl.ANY)] * 3,
        out_specs=pl.BlockSpec(memory_space=pltpu.VMEM),
        scratch_shapes=[
            pltpu.VMEM((wides * sectors, states, depth, size), jnp.bfloat16),
            pltpu.VMEM((WORK, h, states, depth, size), jnp.bfloat16),
            pltpu.VMEM((WORK, h, states, depth, size), jnp.bfloat16),
            pltpu.VMEM((2 * slots, size, half_size), jnp.bfloat16),
            pltpu.VMEM((2 * slots, size, size), jnp.bfloat16),
            pltpu.VMEM((states, size, size), jnp.float32),
            pltpu.VMEM((h, 2, states, depth, size), jnp.bfloat16),
            pltpu.VMEM((h, 2, states, depth, size), jnp.bfloat16),
            pltpu.VMEM((states, depth, size), jnp.bfloat16),
            pltpu.VMEM((states, depth, size), jnp.bfloat16),
            dma((3,)), dma((2,)), dma((2, slots)), dma((2, slots)),
            dma((WORK, h)), dma((WORK, h)), dma((h,)), dma((h,)), dma((2,)),
        ],
        compiler_params=pltpu.CompilerParams(
            collective_id=0, has_side_effects=True, vmem_limit_bytes=60 * 1024 * 1024
        ),
    )(table, wavefunction, left_ops, right_ops)
    return out[None]


def solution(mesh):
    placed = (
        P("wide", None, "op", None),
        P(("wide", "op"), None, None),
        P(("wide", "op"), None, None),
        P(("wide", "op")),
        P(("wide", "op")),
    )
    return jax.shard_map(
        local, mesh=mesh, in_specs=placed, out_specs=P("wide", None, "op", None), check_vma=False
    )
```

```python
import functools

import jax
import jax.numpy as jnp
from jax import lax
from jax.experimental import pallas as pl
from jax.experimental.pallas import tpu as pltpu
from jax.sharding import PartitionSpec as P

MESH = pl.DeviceIdType.MESH
WORK = 6
BLOCKS = 4


def kernel(
    n, small, wf, lefts, rights, out,
    info, table, rows, outgoing, arrived, left_v, right_0, right_1, right_2, right_3,
    acc, red_out, red_in, swap_out, swap_in,
    local_sem, wide_sem, info_send, info_recv, left_send, left_recv, right_send, right_recv,
    a2a_send, a2a_recv, red_send, red_recv, swap_send, swap_recv,
):
    h = n // 2
    w = lax.axis_index("wide")
    me = lax.axis_index("op")
    side = lax.div(me, h)
    r = lax.rem(me, h)
    base = side * h
    partner = lax.rem(me + h, n)
    sectors, states, depth, size = wf.shape
    slots = lefts.shape[0]
    split = size // 2
    width = size // BLOCKS
    right_v = (right_0, right_1, right_2, right_3)

    def each(count, action):
        def step(k, c):
            action(k)
            return c

        lax.fori_loop(1, count, step, 0)

    barrier = pltpu.get_barrier_semaphore()
    other = 1 - w
    pl.semaphore_signal(barrier, inc=1, device_id=(other, me), device_id_type=MESH)
    each(n, lambda k: pl.semaphore_signal(
        barrier, inc=1, device_id=(w, lax.rem(me + k, n)), device_id_type=MESH))

    my_cols = pl.ds(pl.multiple_of(side * split, split), split)
    away_cols = pl.ds(pl.multiple_of((1 - side) * split, split), split)
    my_sectors = pl.ds(w * sectors, sectors)
    local_copies = [
        pltpu.make_async_copy(wf, rows.at[my_sectors], local_sem.at[0]),
        pltpu.make_async_copy(
            lefts.at[:, :, my_cols], left_v.at[pl.ds(0, slots)], local_sem.at[1]
        ),
    ] + [
        pltpu.make_async_copy(
            rights.at[:, pl.ds(q * width, width), :],
            right_v[q].at[pl.ds(0, slots)], local_sem.at[2 + q],
        )
        for q in range(BLOCKS)
    ]
    for copy in local_copies:
        copy.start()
    info[me] = small[...]
    pl.semaphore_wait(barrier, n)

    def remote(src, dst, ssem, rsem, to):
        return pltpu.make_async_remote_copy(
            src_ref=src, dst_ref=dst, send_sem=ssem, recv_sem=rsem,
            device_id=to, device_id_type=MESH,
        )

    def tell(k, at):
        to = lax.rem(me + k, n)
        row = me if at is None else to
        return remote(small, info.at[row], info_send.at[to], info_recv.at[row], (w, to))

    each(n, lambda k: tell(k, None).start())
    wide_copy = remote(wf, rows.at[my_sectors], wide_sem.at[0], wide_sem.at[1], (other, me))
    wide_copy.start()
    left_copies = [
        remote(
            lefts.at[j, :, away_cols], left_v.at[slots + j],
            left_send.at[j], left_recv.at[j], (w, partner),
        )
        for j in range(slots)
    ]
    right_copies = [
        [
            remote(
                rights.at[j, pl.ds(q * width, width), :], right_v[q].at[slots + j],
                right_send.at[q, j], right_recv.at[q, j], (w, partner),
            )
            for j in range(slots)
        ]
        for q in range(BLOCKS)
    ]
    inner = lax.rem(lax.div(4 * me, n) + 1, 4) >= 2

    def start_ops(blocks):
        for q in blocks:
            for copy in right_copies[q]:
                copy.start()

    for copy in left_copies:
        copy.start()

    @pl.when(inner)
    def _():
        start_ops(range(BLOCKS))
    each(n, lambda k: tell(k, 1).wait_recv())
    to_scalars = pltpu.make_async_copy(info, table, local_sem.at[2 + BLOCKS])
    to_scalars.start()
    to_scalars.wait()
    local_copies[0].wait()
    wide_copy.wait()

    def sector(t, e):
        d = base + e
        p = lax.rem(d + h, n)
        live = table[d, 0, slots]
        if t < 2:
            return table[d, 0, t]
        if t < 4:
            return table[p, 0, t - 2]
        if t == 4:
            return jnp.where(live >= 3, table[d, 0, 2], table[p, 0, 2])
        third = jnp.where(live == 3, table[p, 0, 2], table[p, 0, 3])
        return jnp.where(live >= 4, table[d, 0, 3], third)

    def fill(t):
        def one(e, c):
            outgoing[t, e] = rows[sector(t, e)]
            return c

        lax.fori_loop(0, h, one, 0)
        arrived[t, r] = rows[sector(t, r)]

    def a2a(t, k, incoming=False):
        e = lax.rem(r + k, h)
        at = e if incoming else r
        return remote(
            outgoing.at[t, e], arrived.at[t, at], a2a_send.at[t, e], a2a_recv.at[t, at], (w, base + e)
        )

    for t in range(WORK):
        fill(t)
        if t:
            each(h, lambda k: a2a(t - 1, k).start())
    each(h, lambda k: a2a(WORK - 1, k).start())

    @pl.when(jnp.logical_not(inner))
    def _():
        start_ops(range(BLOCKS))

    def compute(t, at, q, first=False):
        x = arrived[t]
        if depth % 16:
            x = x.astype(jnp.float32)
        x = x.reshape(h * states * depth, size).astype(jnp.bfloat16)
        half = lax.dot_general(
            x, right_v[q][at], (((1,), (1,)), ((), ())), preferred_element_type=jnp.float32
        ).reshape(h, states, depth, width)
        left = left_v[at]
        for s in range(states):
            mid = half[:, s].reshape(h * depth, width).astype(jnp.bfloat16)
            term = jnp.dot(left, mid, preferred_element_type=jnp.float32)
            acc[q, s] = term if first else acc[q, s] + term

    for copy in local_copies[1:]:
        copy.wait()
    for t in range(2):
        each(h, lambda k: a2a(t, k, True).wait_recv())
        for q in range(BLOCKS):
            compute(t, t, q, first=t == 0)
    for t in range(2, WORK):
        each(h, lambda k: a2a(t, k, True).wait_recv())
    for copy in left_copies:
        copy.wait_recv()

    my_live = table[me, 0, slots]
    third = jnp.where(my_live >= 3, 2, slots + 2)
    fourth = jnp.where(my_live >= 4, 3, jnp.where(my_live == 3, slots + 2, slots + 3))

    def red(q, k, incoming=False):
        e = lax.rem(r + k, h)
        at = e if incoming else r
        return remote(
            red_out.at[q, e], red_in.at[q, at], red_send.at[q, e], red_recv.at[q, at], (w, base + e)
        )

    def swap(q):
        return remote(swap_out.at[q], swap_in.at[q], swap_send.at[q], swap_recv.at[q], (w, partner))

    def mine(q, p):
        at = pl.ds(pl.multiple_of((p * h + r) * depth, depth), depth)

        def add(k, total):
            return total + red_in[q, lax.rem(r + k, h), p].astype(jnp.float32)

        return lax.fori_loop(1, h, add, acc[q, :, at, :])

    def finish(q):
        each(h, lambda k: red(q, k, True).wait_recv())
        swap_out[q] = mine(q, 1 - side).astype(jnp.bfloat16)
        swap(q).start()

    for q in range(BLOCKS):
        for copy in right_copies[q]:
            copy.wait_recv()
        compute(2, slots, q)
        compute(3, slots + 1, q)
        compute(4, third, q)
        compute(5, fourth, q)

        def pack(e, c):
            for p in range(2):
                at = pl.ds(pl.multiple_of((p * h + e) * depth, depth), depth)
                red_out[q, e, p] = acc[q, :, at, :].astype(jnp.bfloat16)
            return c

        lax.fori_loop(0, h, pack, 0)
        each(h, lambda k: red(q, k).start())
        if q:
            finish(q - 1)
    finish(BLOCKS - 1)
    for q in range(BLOCKS):
        kept = mine(q, side)
        swap(q).wait()
        out[:, :, pl.ds(q * width, width)] = (kept + swap_in[q].astype(jnp.float32)).astype(jnp.bfloat16)
    for t in range(WORK):
        each(h, lambda k: a2a(t, k).wait_send())
    for q in range(BLOCKS):
        each(h, lambda k: red(q, k).wait_send())
        for copy in right_copies[q]:
            copy.wait_send()
    for copy in left_copies:
        copy.wait_send()
    each(n, lambda k: tell(k, None).wait_send())


def local(wavefunction, left_ops, right_ops, in_sector, live_count):
    n, wides = lax.axis_size("op"), lax.axis_size("wide")
    h = n // 2
    slots, size = left_ops.shape[0], left_ops.shape[1]
    sectors, states, depth, _ = wavefunction.shape
    width = size // BLOCKS
    small = jnp.concatenate([in_sector, live_count])
    small = jnp.pad(small, (0, 128 - small.shape[0]))[None]
    dma = pltpu.SemaphoreType.DMA
    bf16, f32 = jnp.bfloat16, jnp.float32
    out = pl.pallas_call(
        functools.partial(kernel, n),
        out_shape=jax.ShapeDtypeStruct((states, depth, size), bf16),
        in_specs=[pl.BlockSpec(memory_space=pltpu.VMEM)]
        + [pl.BlockSpec(memory_space=pl.ANY)] * 3,
        out_specs=pl.BlockSpec(memory_space=pltpu.VMEM),
        scratch_shapes=[
            pltpu.VMEM((n, 1, 128), jnp.int32),
            pltpu.SMEM((n, 1, 128), jnp.int32),
            pltpu.VMEM((wides * sectors, states, depth, size), bf16),
            pltpu.VMEM((WORK, h, states, depth, size), bf16),
            pltpu.VMEM((WORK, h, states, depth, size), bf16),
            pltpu.VMEM((2 * slots, size, size // 2), bf16),
        ]
        + [pltpu.VMEM((2 * slots, width, size), bf16) for q in range(BLOCKS)]
        + [
            pltpu.VMEM((BLOCKS, states, size, width), f32),
            pltpu.VMEM((BLOCKS, h, 2, states, depth, width), bf16),
            pltpu.VMEM((BLOCKS, h, 2, states, depth, width), bf16),
            pltpu.VMEM((BLOCKS, states, depth, width), bf16),
            pltpu.VMEM((BLOCKS, states, depth, width), bf16),
            dma((3 + BLOCKS,)), dma((2,)), dma((n,)), dma((n,)), dma((slots,)), dma((slots,)),
            dma((BLOCKS, slots)), dma((BLOCKS, slots)), dma((WORK, h)), dma((WORK, h)),
            dma((BLOCKS, h)), dma((BLOCKS, h)), dma((BLOCKS,)), dma((BLOCKS,)),
        ],
        compiler_params=pltpu.CompilerParams(
            collective_id=0, has_side_effects=True, vmem_limit_bytes=60 * 1024 * 1024
        ),
    )(small, wavefunction, left_ops, right_ops)
    return out[None]


def solution(mesh):
    placed = (
        P("wide", None, "op", None),
        P(("wide", "op"), None, None),
        P(("wide", "op"), None, None),
        P(("wide", "op")),
        P(("wide", "op")),
    )
    return jax.shard_map(
        local, mesh=mesh, in_specs=placed, out_specs=P("wide", None, "op", None), check_vma=False
    )
```

```python
import functools

import jax
import jax.numpy as jnp
from jax import lax
from jax.experimental import pallas as pl
from jax.experimental.pallas import tpu as pltpu
from jax.sharding import PartitionSpec as P

MESH = pl.DeviceIdType.MESH
WORK = 6
BLOCKS = 4


def kernel(
    n, small, wf, lefts, rights, out,
    info, table, rows, outgoing, arrived, left_v, right_0, right_1, right_2, right_3,
    acc, red_out, red_in, mid_out, mid_in, swap_out, swap_in,
    local_sem, wide_sem, info_send, info_recv, left_send, left_recv, right_send, right_recv,
    a2a_send, a2a_recv, red_send, red_recv, mid_send, mid_recv, swap_send, swap_recv,
):
    h = n // 2
    w = lax.axis_index("wide")
    me = lax.axis_index("op")
    side = lax.div(me, h)
    r = lax.rem(me, h)
    base = side * h
    partner = lax.rem(me + h, n)
    sectors, states, depth, size = wf.shape
    slots = lefts.shape[0]
    split = size // 2
    width = size // BLOCKS
    plane = n // 4
    z = lax.div(me, plane)
    rp = lax.rem(me, plane)
    zl = lax.rem(z, 2)
    neighbour = base + lax.rem(r + plane, h)
    right_v = (right_0, right_1, right_2, right_3)

    def each(count, action):
        def step(k, c):
            action(k)
            return c

        lax.fori_loop(1, count, step, 0)

    barrier = pltpu.get_barrier_semaphore()
    other = 1 - w
    pl.semaphore_signal(barrier, inc=1, device_id=(other, me), device_id_type=MESH)
    each(n, lambda k: pl.semaphore_signal(
        barrier, inc=1, device_id=(w, lax.rem(me + k, n)), device_id_type=MESH))

    my_cols = pl.ds(pl.multiple_of(side * split, split), split)
    away_cols = pl.ds(pl.multiple_of((1 - side) * split, split), split)
    my_sectors = pl.ds(w * sectors, sectors)
    local_copies = [
        pltpu.make_async_copy(wf, rows.at[my_sectors], local_sem.at[0]),
        pltpu.make_async_copy(
            lefts.at[:, :, my_cols], left_v.at[pl.ds(0, slots)], local_sem.at[1]
        ),
    ] + [
        pltpu.make_async_copy(
            rights.at[:, pl.ds(q * width, width), :],
            right_v[q].at[pl.ds(0, slots)], local_sem.at[2 + q],
        )
        for q in range(BLOCKS)
    ]
    for copy in local_copies:
        copy.start()
    info[me] = small[...]
    pl.semaphore_wait(barrier, n)

    def remote(src, dst, ssem, rsem, to):
        return pltpu.make_async_remote_copy(
            src_ref=src, dst_ref=dst, send_sem=ssem, recv_sem=rsem,
            device_id=to, device_id_type=MESH,
        )

    def tell(k, at):
        to = lax.rem(me + k, n)
        row = me if at is None else to
        return remote(small, info.at[row], info_send.at[to], info_recv.at[row], (w, to))

    each(n, lambda k: tell(k, None).start())
    wide_copy = remote(wf, rows.at[my_sectors], wide_sem.at[0], wide_sem.at[1], (other, me))
    wide_copy.start()
    left_copies = [
        remote(
            lefts.at[j, :, away_cols], left_v.at[slots + j],
            left_send.at[j], left_recv.at[j], (w, partner),
        )
        for j in range(slots)
    ]
    right_copies = [
        [
            remote(
                rights.at[j, pl.ds(q * width, width), :], right_v[q].at[slots + j],
                right_send.at[q, j], right_recv.at[q, j], (w, partner),
            )
            for j in range(slots)
        ]
        for q in range(BLOCKS)
    ]
    inner = lax.rem(lax.div(4 * me, n) + 1, 4) >= 2

    def start_ops(blocks):
        for q in blocks:
            for copy in right_copies[q]:
                copy.start()

    for copy in left_copies:
        copy.start()

    @pl.when(inner)
    def _():
        start_ops(range(BLOCKS))
    each(n, lambda k: tell(k, 1).wait_recv())
    to_scalars = pltpu.make_async_copy(info, table, local_sem.at[2 + BLOCKS])
    to_scalars.start()
    to_scalars.wait()
    local_copies[0].wait()
    wide_copy.wait()

    def sector(t, e):
        d = base + e
        p = lax.rem(d + h, n)
        live = table[d, 0, slots]
        if t < 2:
            return table[d, 0, t]
        if t < 4:
            return table[p, 0, t - 2]
        if t == 4:
            return jnp.where(live >= 3, table[d, 0, 2], table[p, 0, 2])
        third = jnp.where(live == 3, table[p, 0, 2], table[p, 0, 3])
        return jnp.where(live >= 4, table[d, 0, 3], third)

    def fill(t):
        def one(e, c):
            outgoing[t, e] = rows[sector(t, e)]
            return c

        lax.fori_loop(0, h, one, 0)
        arrived[t, r] = rows[sector(t, r)]

    def a2a(t, k, incoming=False):
        e = lax.rem(r + k, h)
        at = e if incoming else r
        return remote(
            outgoing.at[t, e], arrived.at[t, at], a2a_send.at[t, e], a2a_recv.at[t, at], (w, base + e)
        )

    for t in range(WORK):
        fill(t)
        if t:
            each(h, lambda k: a2a(t - 1, k).start())
    each(h, lambda k: a2a(WORK - 1, k).start())

    @pl.when(jnp.logical_not(inner))
    def _():
        start_ops(range(BLOCKS))

    def compute(t, at, q, first=False):
        x = arrived[t]
        if depth % 16:
            x = x.astype(jnp.float32)
        x = x.reshape(h * states * depth, size).astype(jnp.bfloat16)
        half = lax.dot_general(
            x, right_v[q][at], (((1,), (1,)), ((), ())), preferred_element_type=jnp.float32
        ).reshape(h, states, depth, width)
        left = left_v[at]
        for s in range(states):
            mid = half[:, s].reshape(h * depth, width).astype(jnp.bfloat16)
            term = jnp.dot(left, mid, preferred_element_type=jnp.float32)
            acc[q, s] = term if first else acc[q, s] + term

    for copy in local_copies[1:]:
        copy.wait()
    for t in range(2):
        each(h, lambda k: a2a(t, k, True).wait_recv())
        for q in range(BLOCKS):
            compute(t, t, q, first=t == 0)
    for t in range(2, WORK):
        each(h, lambda k: a2a(t, k, True).wait_recv())
    for copy in left_copies:
        copy.wait_recv()

    my_live = table[me, 0, slots]
    third = jnp.where(my_live >= 3, 2, slots + 2)
    fourth = jnp.where(my_live >= 4, 3, jnp.where(my_live == 3, slots + 2, slots + 3))

    def red(q, k, incoming=False):
        e = lax.rem(rp + k, plane)
        at = e if incoming else rp
        return remote(
            red_out.at[q, e], red_in.at[q, at], red_send.at[q, e], red_recv.at[q, at],
            (w, z * plane + e),
        )

    def step(q):
        return remote(mid_out.at[q], mid_in.at[q], mid_send.at[q], mid_recv.at[q], (w, neighbour))

    def swap(q):
        return remote(swap_out.at[q], swap_in.at[q], swap_send.at[q], swap_recv.at[q], (w, partner))

    def mine(q, zo):
        at = pl.ds(pl.multiple_of((zo * plane + rp) * depth, depth), depth)

        def add(k, total):
            return total + red_in[q, lax.rem(rp + k, plane), zo].astype(jnp.float32)

        return lax.fori_loop(1, plane, add, acc[q, :, at, :])

    def second(q):
        each(plane, lambda k: red(q, k, True).wait_recv())
        for p in range(2):
            mid_out[q, p] = mine(q, 2 * p + 1 - zl).astype(jnp.bfloat16)
        step(q).start()

    def both(q, p):
        return mine(q, 2 * p + zl) + mid_in[q, p].astype(jnp.float32)

    def third_step(q):
        step(q).wait_recv()
        swap_out[q] = both(q, 1 - side).astype(jnp.bfloat16)
        swap(q).start()

    for q in range(BLOCKS):
        for copy in right_copies[q]:
            copy.wait_recv()
        compute(2, slots, q)
        compute(3, slots + 1, q)
        compute(4, third, q)
        compute(5, fourth, q)

        def pack(e, c):
            for zo in range(4):
                at = pl.ds(pl.multiple_of((zo * plane + e) * depth, depth), depth)
                red_out[q, e, zo] = acc[q, :, at, :].astype(jnp.bfloat16)
            return c

        lax.fori_loop(0, plane, pack, 0)
        each(plane, lambda k: red(q, k).start())
        if q:
            second(q - 1)
        if q > 1:
            third_step(q - 2)
    second(BLOCKS - 1)
    for q in range(max(0, BLOCKS - 2), BLOCKS):
        third_step(q)
    for q in range(BLOCKS):
        kept = both(q, side)
        swap(q).wait()
        out[:, :, pl.ds(q * width, width)] = (kept + swap_in[q].astype(jnp.float32)).astype(jnp.bfloat16)
    for t in range(WORK):
        each(h, lambda k: a2a(t, k).wait_send())
    for q in range(BLOCKS):
        each(plane, lambda k: red(q, k).wait_send())
        step(q).wait_send()
        for copy in right_copies[q]:
            copy.wait_send()
    for copy in left_copies:
        copy.wait_send()
    each(n, lambda k: tell(k, None).wait_send())


def local(wavefunction, left_ops, right_ops, in_sector, live_count):
    n, wides = lax.axis_size("op"), lax.axis_size("wide")
    h = n // 2
    slots, size = left_ops.shape[0], left_ops.shape[1]
    sectors, states, depth, _ = wavefunction.shape
    width = size // BLOCKS
    small = jnp.concatenate([in_sector, live_count])
    small = jnp.pad(small, (0, 128 - small.shape[0]))[None]
    dma = pltpu.SemaphoreType.DMA
    bf16, f32 = jnp.bfloat16, jnp.float32
    out = pl.pallas_call(
        functools.partial(kernel, n),
        out_shape=jax.ShapeDtypeStruct((states, depth, size), bf16),
        in_specs=[pl.BlockSpec(memory_space=pltpu.VMEM)]
        + [pl.BlockSpec(memory_space=pl.ANY)] * 3,
        out_specs=pl.BlockSpec(memory_space=pltpu.VMEM),
        scratch_shapes=[
            pltpu.VMEM((n, 1, 128), jnp.int32),
            pltpu.SMEM((n, 1, 128), jnp.int32),
            pltpu.VMEM((wides * sectors, states, depth, size), bf16),
            pltpu.VMEM((WORK, h, states, depth, size), bf16),
            pltpu.VMEM((WORK, h, states, depth, size), bf16),
            pltpu.VMEM((2 * slots, size, size // 2), bf16),
        ]
        + [pltpu.VMEM((2 * slots, width, size), bf16) for q in range(BLOCKS)]
        + [
            pltpu.VMEM((BLOCKS, states, size, width), f32),
            pltpu.VMEM((BLOCKS, n // 4, 4, states, depth, width), bf16),
            pltpu.VMEM((BLOCKS, n // 4, 4, states, depth, width), bf16),
            pltpu.VMEM((BLOCKS, 2, states, depth, width), bf16),
            pltpu.VMEM((BLOCKS, 2, states, depth, width), bf16),
            pltpu.VMEM((BLOCKS, states, depth, width), bf16),
            pltpu.VMEM((BLOCKS, states, depth, width), bf16),
            dma((3 + BLOCKS,)), dma((2,)), dma((n,)), dma((n,)), dma((slots,)), dma((slots,)),
            dma((BLOCKS, slots)), dma((BLOCKS, slots)), dma((WORK, h)), dma((WORK, h)),
            dma((BLOCKS, n // 4)), dma((BLOCKS, n // 4)),
            dma((BLOCKS,)), dma((BLOCKS,)), dma((BLOCKS,)), dma((BLOCKS,)),
        ],
        compiler_params=pltpu.CompilerParams(
            collective_id=0, has_side_effects=True, vmem_limit_bytes=60 * 1024 * 1024
        ),
    )(small, wavefunction, left_ops, right_ops)
    return out[None]


def solution(mesh):
    placed = (
        P("wide", None, "op", None),
        P(("wide", "op"), None, None),
        P(("wide", "op"), None, None),
        P(("wide", "op")),
        P(("wide", "op")),
    )
    return jax.shard_map(
        local, mesh=mesh, in_specs=placed, out_specs=P("wide", None, "op", None), check_vma=False
    )
```

```python
import functools

import jax
import jax.numpy as jnp
from jax import lax
from jax.experimental import pallas as pl
from jax.experimental.pallas import tpu as pltpu
from jax.sharding import PartitionSpec as P

MESH = pl.DeviceIdType.MESH
WORK = 6
BLOCKS = 4


def kernel(
    n, small, wf, lefts, rights, out,
    info, table, rows, far, outgoing, arrived, left_v, right_0, right_1, right_2, right_3,
    acc, red_out, red_in, mid_out, mid_in, swap_out, swap_in,
    local_sem, wide_sem, info_send, info_recv, left_send, left_recv, right_send, right_recv,
    a2a_send, a2a_recv, red_send, red_recv, mid_send, mid_recv, swap_send, swap_recv,
):
    h = n // 2
    w = lax.axis_index("wide")
    me = lax.axis_index("op")
    side = lax.div(me, h)
    r = lax.rem(me, h)
    base = side * h
    partner = lax.rem(me + h, n)
    sectors, states, depth, size = wf.shape
    slots = lefts.shape[0]
    split = size // 2
    width = size // BLOCKS
    plane = n // 4
    z = lax.div(me, plane)
    rp = lax.rem(me, plane)
    zl = lax.rem(z, 2)
    neighbour = base + lax.rem(r + plane, h)
    right_v = (right_0, right_1, right_2, right_3)

    def each(count, action):
        def step(k, c):
            action(k)
            return c

        lax.fori_loop(1, count, step, 0)

    barrier = pltpu.get_barrier_semaphore()
    other = 1 - w
    pl.semaphore_signal(barrier, inc=1, device_id=(other, me), device_id_type=MESH)
    each(n, lambda k: pl.semaphore_signal(
        barrier, inc=1, device_id=(w, lax.rem(me + k, n)), device_id_type=MESH))

    my_cols = pl.ds(pl.multiple_of(side * split, split), split)
    away_cols = pl.ds(pl.multiple_of((1 - side) * split, split), split)
    my_sectors = pl.ds(w * sectors, sectors)
    local_copies = [
        pltpu.make_async_copy(wf, rows.at[my_sectors], local_sem.at[0]),
        pltpu.make_async_copy(
            lefts.at[:, :, my_cols], left_v.at[pl.ds(0, slots)], local_sem.at[1]
        ),
    ] + [
        pltpu.make_async_copy(
            rights.at[:, pl.ds(q * width, width), :],
            right_v[q].at[pl.ds(0, slots)], local_sem.at[2 + q],
        )
        for q in range(BLOCKS)
    ]
    for copy in local_copies:
        copy.start()
    info[me] = small[...]
    pl.semaphore_wait(barrier, n)

    def remote(src, dst, ssem, rsem, to):
        return pltpu.make_async_remote_copy(
            src_ref=src, dst_ref=dst, send_sem=ssem, recv_sem=rsem,
            device_id=to, device_id_type=MESH,
        )

    def tell(k, at):
        to = lax.rem(me + k, n)
        row = me if at is None else to
        return remote(small, info.at[row], info_send.at[to], info_recv.at[row], (w, to))

    each(n, lambda k: tell(k, None).start())
    wide_copy = remote(wf, rows.at[my_sectors], wide_sem.at[0], wide_sem.at[1], (other, me))
    slab = remote(wf, far.at[my_sectors], wide_sem.at[2], wide_sem.at[3], (w, neighbour))
    slab.start()
    wide_copy.start()
    relay = remote(
        far.at[my_sectors], far.at[my_sectors], wide_sem.at[4], wide_sem.at[5], (other, me)
    )
    left_copies = [
        remote(
            lefts.at[j, :, away_cols], left_v.at[slots + j],
            left_send.at[j], left_recv.at[j], (w, partner),
        )
        for j in range(slots)
    ]
    right_copies = [
        [
            remote(
                rights.at[j, pl.ds(q * width, width), :], right_v[q].at[slots + j],
                right_send.at[q, j], right_recv.at[q, j], (w, partner),
            )
            for j in range(slots)
        ]
        for q in range(BLOCKS)
    ]
    for copy in left_copies:
        copy.start()
    for block in right_copies:
        for copy in block:
            copy.start()

    each(n, lambda k: tell(k, 1).wait_recv())
    to_scalars = pltpu.make_async_copy(info, table, local_sem.at[2 + BLOCKS])
    to_scalars.start()
    to_scalars.wait()
    local_copies[0].wait()
    wide_copy.wait()

    def sector(t, e):
        d = base + e
        p = lax.rem(d + h, n)
        live = table[d, 0, slots]
        if t < 2:
            return table[d, 0, t]
        if t < 4:
            return table[p, 0, t - 2]
        if t == 4:
            return jnp.where(live >= 3, table[d, 0, 2], table[p, 0, 2])
        third = jnp.where(live == 3, table[p, 0, 2], table[p, 0, 3])
        return jnp.where(live >= 4, table[d, 0, 3], third)

    def fill(t, near):
        held, at = (rows, zl) if near else (far, 1 - zl)

        def one(e, c):
            outgoing[t, at * plane + e] = held[sector(t, zl * plane + e)]
            return c

        lax.fori_loop(0, plane, one, 0)
        arrived[t, at * plane + rp] = held[sector(t, r)]

    def a2a(t, near, k, incoming=False):
        e = lax.rem(rp + k, plane)
        held = (zl if near else 1 - zl) * plane
        at = held + (e if incoming else rp)
        return remote(
            outgoing.at[t, held + e], arrived.at[t, at], a2a_send.at[t, held + e], a2a_recv.at[t, at],
            (w, z * plane + e),
        )

    def arrive(t):
        for near in (True, False):
            each(plane, lambda k: a2a(t, near, k, True).wait_recv())

    def send_all(near):
        for t in range(WORK):
            fill(t, near)
            if t:
                each(plane, lambda k: a2a(t - 1, near, k).start())
        each(plane, lambda k: a2a(WORK - 1, near, k).start())

    send_all(True)
    slab.wait_recv()
    relay.start()
    relay.wait()
    send_all(False)

    def compute(t, at, q, first=False):
        x = arrived[t]
        if depth % 16:
            x = x.astype(jnp.float32)
        x = x.reshape(h * states * depth, size).astype(jnp.bfloat16)
        half = lax.dot_general(
            x, right_v[q][at], (((1,), (1,)), ((), ())), preferred_element_type=jnp.float32
        ).reshape(h, states, depth, width)
        left = left_v[at]
        for s in range(states):
            mid = half[:, s].reshape(h * depth, width).astype(jnp.bfloat16)
            term = jnp.dot(left, mid, preferred_element_type=jnp.float32)
            acc[q, s] = term if first else acc[q, s] + term

    for copy in local_copies[1:]:
        copy.wait()
    for t in range(2):
        arrive(t)
        for q in range(BLOCKS):
            compute(t, t, q, first=t == 0)
    for t in range(2, WORK):
        arrive(t)
    for copy in left_copies:
        copy.wait_recv()

    my_live = table[me, 0, slots]
    third = jnp.where(my_live >= 3, 2, slots + 2)
    fourth = jnp.where(my_live >= 4, 3, jnp.where(my_live == 3, slots + 2, slots + 3))

    def red(q, k, incoming=False):
        e = lax.rem(rp + k, plane)
        at = e if incoming else rp
        return remote(
            red_out.at[q, e], red_in.at[q, at], red_send.at[q, e], red_recv.at[q, at],
            (w, z * plane + e),
        )

    def step(q):
        return remote(mid_out.at[q], mid_in.at[q], mid_send.at[q], mid_recv.at[q], (w, neighbour))

    def swap(q):
        return remote(swap_out.at[q], swap_in.at[q], swap_send.at[q], swap_recv.at[q], (w, partner))

    def mine(q, zo):
        at = pl.ds(pl.multiple_of((zo * plane + rp) * depth, depth), depth)

        def add(k, total):
            return total + red_in[q, lax.rem(rp + k, plane), zo].astype(jnp.float32)

        return lax.fori_loop(1, plane, add, acc[q, :, at, :])

    def second(q):
        each(plane, lambda k: red(q, k, True).wait_recv())
        for p in range(2):
            mid_out[q, p] = mine(q, 2 * p + 1 - zl).astype(jnp.bfloat16)
        step(q).start()

    def both(q, p):
        return mine(q, 2 * p + zl) + mid_in[q, p].astype(jnp.float32)

    def third_step(q):
        step(q).wait_recv()
        swap_out[q] = both(q, 1 - side).astype(jnp.bfloat16)
        swap(q).start()

    for q in range(BLOCKS):
        for copy in right_copies[q]:
            copy.wait_recv()
        compute(2, slots, q)
        compute(3, slots + 1, q)
        compute(4, third, q)
        compute(5, fourth, q)

        def pack(e, c):
            for zo in range(4):
                at = pl.ds(pl.multiple_of((zo * plane + e) * depth, depth), depth)
                red_out[q, e, zo] = acc[q, :, at, :].astype(jnp.bfloat16)
            return c

        lax.fori_loop(0, plane, pack, 0)
        each(plane, lambda k: red(q, k).start())
        if q:
            second(q - 1)
        if q > 1:
            third_step(q - 2)
    second(BLOCKS - 1)
    for q in range(max(0, BLOCKS - 2), BLOCKS):
        third_step(q)
    for q in range(BLOCKS):
        kept = both(q, side)
        swap(q).wait()
        out[:, :, pl.ds(q * width, width)] = (kept + swap_in[q].astype(jnp.float32)).astype(jnp.bfloat16)
    for t in range(WORK):
        for near in (True, False):
            each(plane, lambda k: a2a(t, near, k).wait_send())
    for q in range(BLOCKS):
        each(plane, lambda k: red(q, k).wait_send())
        step(q).wait_send()
        for copy in right_copies[q]:
            copy.wait_send()
    for copy in left_copies:
        copy.wait_send()
    each(n, lambda k: tell(k, None).wait_send())
    slab.wait_send()


def local(wavefunction, left_ops, right_ops, in_sector, live_count):
    n, wides = lax.axis_size("op"), lax.axis_size("wide")
    h = n // 2
    slots, size = left_ops.shape[0], left_ops.shape[1]
    sectors, states, depth, _ = wavefunction.shape
    width = size // BLOCKS
    small = jnp.concatenate([in_sector, live_count])
    small = jnp.pad(small, (0, 128 - small.shape[0]))[None]
    dma = pltpu.SemaphoreType.DMA
    bf16, f32 = jnp.bfloat16, jnp.float32
    out = pl.pallas_call(
        functools.partial(kernel, n),
        out_shape=jax.ShapeDtypeStruct((states, depth, size), bf16),
        in_specs=[pl.BlockSpec(memory_space=pltpu.VMEM)]
        + [pl.BlockSpec(memory_space=pl.ANY)] * 3,
        out_specs=pl.BlockSpec(memory_space=pltpu.VMEM),
        scratch_shapes=[
            pltpu.VMEM((n, 1, 128), jnp.int32),
            pltpu.SMEM((n, 1, 128), jnp.int32),
            pltpu.VMEM((wides * sectors, states, depth, size), bf16),
            pltpu.VMEM((wides * sectors, states, depth, size), bf16),
            pltpu.VMEM((WORK, h, states, depth, size), bf16),
            pltpu.VMEM((WORK, h, states, depth, size), bf16),
            pltpu.VMEM((2 * slots, size, size // 2), bf16),
        ]
        + [pltpu.VMEM((2 * slots, width, size), bf16) for q in range(BLOCKS)]
        + [
            pltpu.VMEM((BLOCKS, states, size, width), f32),
            pltpu.VMEM((BLOCKS, n // 4, 4, states, depth, width), bf16),
            pltpu.VMEM((BLOCKS, n // 4, 4, states, depth, width), bf16),
            pltpu.VMEM((BLOCKS, 2, states, depth, width), bf16),
            pltpu.VMEM((BLOCKS, 2, states, depth, width), bf16),
            pltpu.VMEM((BLOCKS, states, depth, width), bf16),
            pltpu.VMEM((BLOCKS, states, depth, width), bf16),
            dma((3 + BLOCKS,)), dma((6,)), dma((n,)), dma((n,)), dma((slots,)), dma((slots,)),
            dma((BLOCKS, slots)), dma((BLOCKS, slots)), dma((WORK, h)), dma((WORK, h)),
            dma((BLOCKS, n // 4)), dma((BLOCKS, n // 4)),
            dma((BLOCKS,)), dma((BLOCKS,)), dma((BLOCKS,)), dma((BLOCKS,)),
        ],
        compiler_params=pltpu.CompilerParams(
            collective_id=0, has_side_effects=True, vmem_limit_bytes=60 * 1024 * 1024
        ),
    )(small, wavefunction, left_ops, right_ops)
    return out[None]


def solution(mesh):
    placed = (
        P("wide", None, "op", None),
        P(("wide", "op"), None, None),
        P(("wide", "op"), None, None),
        P(("wide", "op")),
        P(("wide", "op")),
    )
    return jax.shard_map(
        local, mesh=mesh, in_specs=placed, out_specs=P("wide", None, "op", None), check_vma=False
    )
```
